32 devices in a mesh: grp: 4 (over y, core), dev: 8 (over z, x).
Axes of the slice: x: 2, y: 2, z: 4, core: 2. Of those that a mesh axis runs over, the one named last changes fastest.
Arguments:
- tokens: bfloat16 [4096, 2048], P(('grp', 'dev')), may hold values from -6 to 6
- cotangent: bfloat16 [4096, 2048], P(('grp', 'dev')), may hold values from -1.5 to 1.5
- route_weight: float32 [4096, 2], P(('grp', 'dev')), may hold values from 0.1 to 1
- slot_expert: int32 [32], replicated, may hold values from 0 to 15, as said below
- targets: int32 [4096, 2], P(('grp', 'dev')), may hold values from 0 to 31, as said below
- proj_in: float32 [16, 2048, 2048], P('grp', 'dev'), may hold values from -0.125 to 0.125
- first_in: float32 [16, 2048, 2048], P('grp', 'dev'), may hold values from -6 to 6
- second_in: float32 [16, 2048, 2048], P('grp', 'dev'), may hold values from 0.01 to 1
- proj_out: float32 [16, 1024, 2048], P('grp', 'dev'), may hold values from -0.1875 to 0.1875
- first_out: float32 [16, 1024, 2048], P('grp', 'dev'), may hold values from -6 to 6
- second_out: float32 [16, 1024, 2048], P('grp', 'dev'), may hold values from 0.01 to 1
Outputs:
- mixed: bfloat16 [4096, 2048], P(('grp', 'dev'))
- token_grad: bfloat16 [4096, 2048], P(('grp', 'dev'))
- mix_grad: float32 [4096, 2], P(('grp', 'dev'))
- trained_in: float32 [16, 2048, 2048], P('grp', 'dev')
- mean_in: float32 [16, 2048, 2048], P('grp', 'dev')
- square_in: float32 [16, 2048, 2048], P('grp', 'dev')
- trained_out: float32 [16, 1024, 2048], P('grp', 'dev')
- mean_out: float32 [16, 1024, 2048], P('grp', 'dev')
- square_out: float32 [16, 1024, 2048], P('grp', 'dev')
The draws below stay inside these ranges and needn't reach their ends.
Inputs may be any that keep to these rules, and one draw needn't show every extreme that they name: `slot_expert`: entry s is the expert held by slot s, the device s in grp+dev order; each of the 16 experts is held by at least one slot. `targets`: entry [t, k] is the slot that serves the k-th expert of token t; the two slots of a token hold different experts.
All inputs are finite; a program needn't handle non-finite values.
Results may differ from the reference program's by a relative error of at most 0.015.
The reference program's roundings to bfloat16 on the way count: a program that leaves them out, or rounds other values in their place, can miss the bound.
Values may be sent and summed in bfloat16 or wider, within the bound.
A program may use at most 192 MiB of HBM per device.

```python
import math
import jax
import jax.numpy as jnp
from jax import lax

D = 2048
FF = 1024
E = 16
TOK_DEV = 128
SLOTS = 32
TOKENS = 4096
CAP = 12
N_GRP = 4
N_DEV = 8


def route_plan(key):
    folded = jax.random.fold_in(key, 4243)
    subkeys = jax.random.split(folded, 6)
    shuffle = jax.random.permutation(subkeys[0], E)
    first_pick = jax.random.randint(subkeys[1], (SLOTS - E,), 0, E)
    second_pick = jax.random.randint(subkeys[2], (SLOTS - E,), 0, E)
    extras = shuffle[jnp.minimum(first_pick, second_pick)].astype(jnp.int32)
    filled = jnp.concatenate([jnp.arange(E, dtype=jnp.int32), extras])
    reorder = jax.random.permutation(subkeys[3], SLOTS)
    experts = filled[reorder].astype(jnp.int32)
    first_slot = jax.random.randint(subkeys[4], (TOKENS,), 0, SLOTS).astype(jnp.int32)
    first_expert = experts[first_slot]
    differ = (experts[None, :] != first_expert[:, None]).astype(jnp.int32)
    others = jnp.sum(differ, axis=1)
    chosen = jax.random.randint(subkeys[5], (TOKENS,), 0, others).astype(jnp.int32)
    running = jnp.cumsum(differ, axis=1)
    second_slot = jnp.sum((running <= chosen[:, None]).astype(jnp.int32), axis=1)
    return (experts, jnp.stack([first_slot, second_slot], axis=1).astype(jnp.int32))


def draw_slot_expert(key, part):
    return route_plan(key)[0]


def draw_targets(key, part):
    return route_plan(key)[1]


def level_of(stream_key, extent, cuts, low, high):
    gain = 1.0
    for dim, parts in cuts:
        heights = jax.random.uniform(jax.random.fold_in(jax.random.fold_in(stream_key, 6), dim), (parts,), jnp.float32, low / len(cuts), high / len(cuts))
        gain = gain * jnp.repeat(jnp.exp(heights), extent[dim] // parts).reshape((-1,) + (1,) * (len(extent) - 1 - dim))
    return gain


def bell_draw(rng, shape, scale, limit, cuts=(), kind=jnp.bfloat16):
    loudness = level_of(rng, shape, cuts, -0.22, 0.18) if cuts else 1.0
    drawn = jax.random.normal(rng, shape, jnp.float32) * scale * loudness
    return jnp.minimum(jnp.maximum(drawn, -limit), limit).astype(kind)


def setup_inputs(seed: int = 0) -> dict:
    splits = jax.random.split(jax.random.key(seed), 12)
    return {
        "tokens": bell_draw(splits[0], (TOKENS, D), 1.0, 6.0, ((0, 32),)),
        "cotangent": bell_draw(splits[1], (TOKENS, D), 0.25, 1.5, ((0, 32),)),
        "route_weight": jnp.clip(0.1 + 0.9 * jax.random.uniform(splits[2], (TOKENS, 2), jnp.float32) ** level_of(splits[2], (TOKENS, 2), ((0, 32),), -0.2, 0.2), 0.1, 1.0),
        "slot_expert": draw_slot_expert(jax.random.fold_in(splits[11], 71), 0),
        "targets": draw_targets(jax.random.fold_in(splits[11], 71), 0),
        "proj_in": bell_draw(splits[5], (E, D, 2 * FF), D ** -0.5, 0.125, ((0, 4), (1, 8)), jnp.float32),
        "first_in": bell_draw(splits[6], (E, D, 2 * FF), 1.0, 6.0, ((0, 4), (1, 8)), jnp.float32),
        "second_in": jnp.clip(jnp.exp(math.log(1.0) - 4.6051702 * jax.random.uniform(splits[7], (E, D, 2 * FF), jnp.float32) ** level_of(splits[7], (E, D, 2 * FF), ((0, 4), (1, 8)), -0.2, 0.2)), 0.01, 1.0),
        "proj_out": bell_draw(splits[8], (E, FF, D), FF ** -0.5, 0.1875, ((0, 4), (1, 8)), jnp.float32),
        "first_out": bell_draw(splits[9], (E, FF, D), 1.0, 6.0, ((0, 4), (1, 8)), jnp.float32),
        "second_out": jnp.clip(jnp.exp(math.log(1.0) - 4.6051702 * jax.random.uniform(splits[10], (E, FF, D), jnp.float32) ** level_of(splits[10], (E, FF, D), ((0, 4), (1, 8)), -0.2, 0.2)), 0.01, 1.0),
    }


beta_first = 0.9
beta_second = 0.95
learn_rate = 0.01
decay_rate = 0.1
adam_eps = 1e-08
bias_first = 1.0 - 0.9 ** 10
bias_second = 1.0 - 0.95 ** 10

def silu_parts(values):
    logistic = jax.nn.sigmoid(values)
    return (values * logistic, logistic * (1.0 + values * (1.0 - logistic)))

def slot_pass(rows_x, rows_dy, weight_up, weight_down):
    gate_up = jnp.dot(rows_x, weight_up, preferred_element_type=jnp.float32)
    gating = gate_up[:, :FF]
    upward = gate_up[:, FF:]
    active, derivative = silu_parts(gating)
    hidden = (active * upward).astype(jnp.bfloat16)
    result = jnp.dot(hidden, weight_down, preferred_element_type=jnp.float32).astype(jnp.bfloat16)
    dhidden = lax.dot_general(rows_dy, weight_down, (((1,), (1,)), ((), ())), preferred_element_type=jnp.float32)
    grad_gateup = jnp.concatenate([dhidden * upward * derivative, dhidden * active], axis=1).astype(jnp.bfloat16)
    rows_dx = lax.dot_general(grad_gateup, weight_up, (((1,), (1,)), ((), ())), preferred_element_type=jnp.float32).astype(jnp.bfloat16)
    grad_up = lax.dot_general(rows_x, grad_gateup, (((0,), (0,)), ((), ())), preferred_element_type=jnp.float32).astype(jnp.bfloat16)
    grad_down = lax.dot_general(hidden, rows_dy, (((0,), (0,)), ((), ())), preferred_element_type=jnp.float32).astype(jnp.bfloat16)
    return (result, rows_dx, grad_up, grad_down)

def adam_step(weight, moment, square, gradient):
    new_moment = beta_first * moment + (1.0 - beta_first) * gradient
    new_square = beta_second * square + (1.0 - beta_second) * gradient * gradient
    update = new_moment / bias_first / (jnp.sqrt(new_square / bias_second) + adam_eps) + decay_rate * weight
    return (weight - learn_rate * update, new_moment, new_square)

def reference(tokens, cotangent, route_weight, slot_expert, targets, proj_in, first_in, second_in, proj_out, first_out, second_out):
    assigns = 2 * TOK_DEV
    buffer_rows = SLOTS * CAP
    per_source = targets.reshape(SLOTS, assigns)
    slot_ids = jnp.arange(SLOTS, dtype=jnp.int32)
    onehot = (per_source[:, :, None] == slot_ids[None, None, :]).astype(jnp.int32)
    earlier = jnp.cumsum(onehot, axis=1) - onehot
    position = lax.optimization_barrier(jnp.sum(earlier * onehot, axis=2)).astype(jnp.int32)
    within = position < CAP
    landing = per_source * buffer_rows + slot_ids[:, None] * CAP + position
    landing = jnp.where(within, landing, SLOTS * buffer_rows).astype(jnp.int32)
    assign_ids = jnp.arange(SLOTS * assigns, dtype=jnp.int32)
    row_table = jnp.full((SLOTS * buffer_rows,), -1, jnp.int32).at[landing.reshape(-1)].set(assign_ids, mode='drop')
    row_table = row_table.reshape(SLOTS, buffer_rows)
    flat_weight = route_weight.reshape(-1)
    scaled = (flat_weight[:, None] * jnp.repeat(cotangent, 2, axis=0).astype(jnp.float32)).astype(jnp.bfloat16)

    def serve_slot(carried, slot_id):
        acc_up, acc_down, out_all, dx_all = carried
        entries = row_table[slot_id]
        filled = entries >= 0
        safe_ids = jnp.where(filled, entries, 0).astype(jnp.int32)
        rows_x = jnp.where(filled[:, None], tokens[safe_ids // 2], jnp.zeros((), tokens.dtype))
        rows_dy = jnp.where(filled[:, None], scaled[safe_ids], jnp.zeros((), scaled.dtype))
        expert = slot_expert[slot_id]
        weight_up = lax.dynamic_index_in_dim(proj_in, expert, 0, keepdims=False).astype(jnp.bfloat16)
        weight_down = lax.dynamic_index_in_dim(proj_out, expert, 0, keepdims=False).astype(jnp.bfloat16)
        result, rows_dx, grad_up, grad_down = slot_pass(rows_x, rows_dy, weight_up, weight_down)
        acc_up = acc_up.at[expert].add(grad_up.astype(jnp.float32))
        acc_down = acc_down.at[expert].add(grad_down.astype(jnp.float32))
        landing_row = jnp.where(filled, entries, 2 * TOKENS).astype(jnp.int32)
        out_all = out_all.at[landing_row].set(result, mode='drop')
        dx_all = dx_all.at[landing_row].set(rows_dx, mode='drop')
        return ((acc_up, acc_down, out_all, dx_all), None)
    total_up = jnp.zeros((E, D, 2 * FF), jnp.float32)
    total_down = jnp.zeros((E, FF, D), jnp.float32)
    out_all = jnp.zeros((2 * TOKENS, D), jnp.bfloat16)
    dx_all = jnp.zeros((2 * TOKENS, D), jnp.bfloat16)
    for group_id in range(N_GRP):
        start_up = jnp.zeros((E, D, 2 * FF), jnp.float32)
        start_down = jnp.zeros((E, FF, D), jnp.float32)
        slot_range = jnp.arange(group_id * N_DEV, (group_id + 1) * N_DEV, dtype=jnp.int32)
        finished, unused = lax.scan(serve_slot, (start_up, start_down, out_all, dx_all), slot_range)
        acc_up, acc_down, out_all, dx_all = finished
        total_up = total_up + lax.optimization_barrier(acc_up.astype(jnp.bfloat16)).astype(jnp.float32)
        total_down = total_down + lax.optimization_barrier(acc_down.astype(jnp.bfloat16)).astype(jnp.float32)
    out_float = out_all.reshape(TOKENS, 2, D).astype(jnp.float32)
    dx_pairs = dx_all.reshape(TOKENS, 2, D).astype(jnp.float32)
    mixed = (route_weight[:, 0:1] * out_float[:, 0] + route_weight[:, 1:2] * out_float[:, 1]).astype(jnp.bfloat16)
    token_grad = (dx_pairs[:, 0] + dx_pairs[:, 1]).astype(jnp.bfloat16)
    mix_grad = lax.optimization_barrier(jnp.sum(cotangent.astype(jnp.float32)[:, None, :] * out_float, axis=2))
    trained_in, mean_in, square_in = adam_step(proj_in, first_in, second_in, total_up)
    trained_out, mean_out, square_out = adam_step(proj_out, first_out, second_out, total_down)
    return (mixed, token_grad, mix_grad, trained_in, mean_in, square_in, trained_out, mean_out, square_out)
```

```python
import jax
import jax.numpy as jnp
from jax import lax
from jax.experimental import pallas as pl
from jax.experimental.pallas import tpu as pltpu
from jax.sharding import PartitionSpec as P

D = 2048
FF = 1024
E = 16


beta_first = 0.9
beta_second = 0.95
learn_rate = 0.01
decay_rate = 0.1
adam_eps = 1e-08
bias_first = 1.0 - 0.9**10
bias_second = 1.0 - 0.95**10


def silu_parts(values):
    logistic = jax.nn.sigmoid(values)
    return (values * logistic, logistic * (1.0 + values * (1.0 - logistic)))


def adam_step(weight, moment, square, gradient):
    new_moment = beta_first * moment + (1.0 - beta_first) * gradient
    new_square = beta_second * square + (1.0 - beta_second) * gradient * gradient
    update = (
        new_moment / bias_first / (jnp.sqrt(new_square / bias_second) + adam_eps)
        + decay_rate * weight
    )
    return (weight - learn_rate * update, new_moment, new_square)


def after(value, *earlier):
    return lax.optimization_barrier((value,) + earlier)[0]


def expert_sums(experts, rows):
    members, depth, width = rows.shape
    tile = 16

    def kernel(expert_ref, rows_ref, out_ref, acc_ref):
        acc_ref[...] = jnp.zeros_like(acc_ref)

        def add(d, carry):
            e = expert_ref[d]
            acc_ref[e] = acc_ref[e] + rows_ref[d].astype(jnp.float32)
            return carry

        lax.fori_loop(0, members, add, 0)
        out_ref[...] = acc_ref[...].astype(out_ref.dtype)

    return pl.pallas_call(
        kernel,
        grid_spec=pltpu.PrefetchScalarGridSpec(
            num_scalar_prefetch=1,
            grid=(depth // tile,),
            in_specs=[pl.BlockSpec((members, tile, width), lambda i, e: (0, i, 0))],
            out_specs=pl.BlockSpec((E, tile, width), lambda i, e: (0, i, 0)),
            scratch_shapes=[pltpu.VMEM((E, tile, width), jnp.float32)],
        ),
        out_shape=jax.ShapeDtypeStruct((E, depth, width), jnp.bfloat16),
        compiler_params=pltpu.CompilerParams(vmem_limit_bytes=24 * 1024 * 1024),
        cost_estimate=pl.CostEstimate(
            flops=members * depth * width,
            bytes_accessed=2 * (members + E) * depth * width,
            transcendentals=0,
        ),
    )(experts, rows)


def pick_experts(stack, experts):
    return jnp.take(stack, experts, axis=0, mode="clip")


def exchange(payload, axes, index_groups=None):
    return lax.all_to_all(
        payload, axes, split_axis=0, concat_axis=0, tiled=True, axis_index_groups=index_groups
    )


def on_device(
    tokens,
    cotangent,
    route_weight,
    slot_expert,
    targets,
    proj_in,
    first_in,
    second_in,
    proj_out,
    first_out,
    second_out,
):
    groups = lax.axis_size("grp")
    members = lax.axis_size("dev")
    slot_count = groups * members
    everyone = ("grp", "dev")
    tok_count = tokens.shape[0]
    capacity = 3 * tok_count // slot_count
    side = members // 2
    pair = 2 * capacity
    pair_rows = slot_count * pair
    slot_rows = slot_count * capacity
    wide = D // 2
    part = FF // 2
    sides = [list(range(side)), list(range(side, members))]
    swap = [(d, (d + side) % members) for d in range(members)]

    my_group = lax.axis_index("grp")
    high = lax.axis_index("dev") >= side
    group_expert = lax.dynamic_slice_in_dim(slot_expert, my_group * members, members)
    group_expert = jnp.clip(group_expert, 0, E - 1)
    pair_expert = group_expert.reshape(2, side).T.reshape(members)

    low_out = proj_out.astype(jnp.bfloat16)
    all_down = lax.all_gather(low_out, "grp", axis=0, tiled=True)
    low_in = proj_in.astype(jnp.bfloat16)
    half = low_in.shape[1] // 2
    all_1 = lax.all_gather(low_in[:, :half], "grp", axis=0, tiled=True)
    all_2 = lax.all_gather(low_in[:, half:], "grp", axis=0, tiled=True)

    flat_target = targets.reshape(-1)
    onehot = (flat_target[:, None] == jnp.arange(slot_count, dtype=jnp.int32)[None, :]).astype(
        jnp.int32
    )
    earlier = jnp.cumsum(onehot, axis=0) - onehot
    position = jnp.sum(earlier * onehot, axis=1)
    within = position < capacity
    member = flat_target % members
    host = flat_target - member + member % side
    row = host * pair + (member // side) * capacity + position
    row = jnp.where(within, row, -2 * pair_rows).reshape(tok_count, 2)
    rows_of = [[row[:, k] + h * side * pair for k in (0, 1)] for h in (0, 1)]
    places = jnp.arange(pair_rows, dtype=jnp.int32)

    def hits(wanted):
        found = places[:, None] == wanted[0][None, :]
        for other in wanted[1:]:
            found = found | (places[:, None] == other[None, :])
        return found

    def takes(wanted):
        found = wanted[0][:, None] == places[None, :]
        for other in wanted[1:]:
            found = found | (other[:, None] == places[None, :])
        return found

    def by_chunk(values):
        split = values.reshape(tok_count, 2, side, 2, half)
        return jnp.swapaxes(split, 2, 3).reshape(tok_count, D)

    def from_chunk(values):
        split = values.reshape(tok_count, 2, 2, side, half)
        return jnp.swapaxes(split, 2, 3).reshape(tok_count, D)

    picker_x = jnp.concatenate([hits(rows_of[0]), hits(rows_of[1])], axis=1).astype(jnp.bfloat16)
    picker_dy = jnp.concatenate(
        [hits([rows_of[0][k], rows_of[1][k]]) for k in (0, 1)], axis=1
    ).astype(jnp.bfloat16)
    cot_float = cotangent.astype(jnp.float32)
    scaled = [(route_weight[:, k : k + 1] * cot_float).astype(jnp.bfloat16) for k in (0, 1)]
    chunked = by_chunk(tokens)
    send_x = jnp.dot(
        picker_x,
        jnp.concatenate([chunked[:, :wide], chunked[:, wide:]], axis=0),
        preferred_element_type=jnp.float32,
    ).astype(jnp.bfloat16)
    send_dy = jnp.dot(
        picker_dy, jnp.concatenate(scaled, axis=0), preferred_element_type=jnp.float32
    ).astype(jnp.bfloat16)
    send = jnp.concatenate([send_x, send_dy], axis=1)
    slot_both = exchange(send.reshape(slot_count, pair, wide + D), everyone)

    got_down = exchange(after(pick_experts(all_down, pair_expert), slot_both), "dev", sides)
    got_1 = exchange(after(pick_experts(all_1, pair_expert), got_down), "dev", sides)
    got_2 = exchange(after(pick_experts(all_2, pair_expert), got_1), "dev", sides)

    def of_slot(got, b):
        rows = got.shape[1]
        return got.reshape(side, 2, rows, got.shape[2])[:, b].reshape(side * rows, got.shape[2])

    across = (((1,), (1,)), ((), ()))
    down = (((0,), (0,)), ((), ()))

    def low_dot(a, b, dims):
        return lax.dot_general(a, b, dims, preferred_element_type=jnp.float32).astype(jnp.bfloat16)

    def pass_over(values):
        return lax.ppermute(values, "dev", swap)

    both = (0, 1)
    quarter = side * half
    slot_x = [slot_both[:, b * capacity : (b + 1) * capacity, :wide].reshape(slot_rows, wide) for b in both]
    slot_dy = [slot_both[:, b * capacity : (b + 1) * capacity, wide:].reshape(slot_rows, D) for b in both]
    x_1 = [x[:, :quarter] for x in slot_x]
    x_2 = [x[:, quarter:] for x in slot_x]
    up_1 = [of_slot(got_1, b) for b in both]
    up_2 = [of_slot(got_2, b) for b in both]
    slot_down = [of_slot(got_down, b) for b in both]

    dhidden = [
        lax.dot_general(slot_dy[b], slot_down[b], across, preferred_element_type=jnp.float32)
        for b in both
    ]
    mine = []
    passed = []
    for b in both:
        total = jnp.dot(x_1[b], up_1[b], preferred_element_type=jnp.float32) + jnp.dot(
            x_2[b], up_2[b], preferred_element_type=jnp.float32
        )
        lower = jnp.concatenate([total[:, :part], total[:, FF : FF + part]], axis=1)
        upper = jnp.concatenate([total[:, part:FF], total[:, FF + part :]], axis=1)
        mine.append(jnp.where(high, upper, lower))
        theirs = jnp.where(high, lower, upper).astype(jnp.bfloat16)
        passed.append(pass_over(theirs))
    hidden = []
    grad_gateup = []
    for b in both:
        gate_up = mine[b] + passed[b].astype(jnp.float32)
        upward = gate_up[:, part:]
        active, derivative = silu_parts(gate_up[:, :part])
        hidden.append((active * upward).astype(jnp.bfloat16))
        own = jnp.concatenate(
            [dhidden[b] * upward * derivative, dhidden[b] * active], axis=1
        ).astype(jnp.bfloat16)
        other = pass_over(own)
        lower = jnp.where(high, other, own)
        upper = jnp.where(high, own, other)
        grad_gateup.append(
            jnp.concatenate(
                [lower[:, :part], upper[:, :part], lower[:, part:], upper[:, part:]], axis=1
            )
        )

    def both_slots(values):
        rows = values[0].shape[0] // side
        return jnp.stack([v.reshape(side, rows, v.shape[1]) for v in values], axis=1).reshape(
            members, rows, values[0].shape[1]
        )

    grad_down = both_slots([low_dot(hidden[b], slot_dy[b], down) for b in both])
    rows_down = exchange(grad_down, "dev", sides)
    result = [low_dot(hidden[b], slot_down[b], (((1,), (0,)), ((), ()))) for b in both]
    grad_1 = both_slots([low_dot(x_1[b], grad_gateup[b], down) for b in both])
    rows_1 = exchange(after(grad_1, rows_down), "dev", sides)
    grad_2 = both_slots([low_dot(x_2[b], grad_gateup[b], down) for b in both])
    rows_2 = exchange(after(grad_2, rows_1), "dev", sides)
    rows_back = [
        jnp.concatenate(
            [
                low_dot(grad_gateup[b], up_1[b], across),
                low_dot(grad_gateup[b], up_2[b], across),
                result[b],
            ],
            axis=1,
        ).reshape(slot_count, capacity, wide + D)
        for b in both
    ]
    back = jnp.concatenate(rows_back, axis=1)
    back = exchange(after(back, rows_2), everyone).reshape(pair_rows, wide + D)
    part_down = expert_sums(pair_expert, rows_down)
    part_1 = expert_sums(pair_expert, rows_1)
    part_2 = expert_sums(pair_expert, rows_2)
    sum_down = lax.psum_scatter(part_down, "grp", scatter_dimension=0, tiled=True)
    sum_1 = lax.psum_scatter(part_1, "grp", scatter_dimension=0, tiled=True)
    sum_2 = lax.psum_scatter(part_2, "grp", scatter_dimension=0, tiled=True)
    sum_up = jnp.concatenate([sum_1, sum_2], axis=1)

    taker = jnp.concatenate(
        [takes([rows_of[0][k], rows_of[1][k]]) for k in (0, 1)], axis=0
    ).astype(jnp.bfloat16)
    taken = jnp.dot(taker, back[:, wide:], preferred_element_type=jnp.float32).astype(jnp.bfloat16)
    out_0 = taken[:tok_count].astype(jnp.float32)
    out_1 = taken[tok_count:].astype(jnp.float32)
    taker_dx = jnp.concatenate([takes(rows_of[0]), takes(rows_of[1])], axis=0).astype(jnp.bfloat16)
    taken_dx = jnp.dot(taker_dx, back[:, :wide], preferred_element_type=jnp.float32)
    mixed = (route_weight[:, 0:1] * out_0 + route_weight[:, 1:2] * out_1).astype(jnp.bfloat16)
    token_grad = from_chunk(
        jnp.concatenate([taken_dx[:tok_count], taken_dx[tok_count:]], axis=1).astype(jnp.bfloat16)
    )
    mix_grad = jnp.stack(
        [jnp.sum(cot_float * out_0, axis=1), jnp.sum(cot_float * out_1, axis=1)], axis=1
    )

    trained_in, mean_in, square_in = adam_step(
        proj_in, first_in, second_in, sum_up.astype(jnp.float32)
    )
    trained_out, mean_out, square_out = adam_step(
        proj_out, first_out, second_out, sum_down.astype(jnp.float32)
    )
    return (
        mixed,
        token_grad,
        mix_grad,
        trained_in,
        mean_in,
        square_in,
        trained_out,
        mean_out,
        square_out,
    )


def solution(mesh):
    in_specs = (
        P(("grp", "dev"), None),
        P(("grp", "dev"), None),
        P(("grp", "dev"), None),
        P(),
        P(("grp", "dev"), None),
        P("grp", "dev", None),
        P("grp", "dev", None),
        P("grp", "dev", None),
        P("grp", "dev", None),
        P("grp", "dev", None),
        P("grp", "dev", None),
    )
    out_specs = (
        P(("grp", "dev"), None),
        P(("grp", "dev"), None),
        P(("grp", "dev"), None),
        P("grp", "dev", None),
        P("grp", "dev", None),
        P("grp", "dev", None),
        P("grp", "dev", None),
        P("grp", "dev", None),
        P("grp", "dev", None),
    )
    return jax.shard_map(
        on_device, mesh=mesh, in_specs=in_specs, out_specs=out_specs, check_vma=False
    )
```

```python
import jax
import jax.numpy as jnp
from jax import lax
from jax.experimental import pallas as pl
from jax.experimental.pallas import tpu as pltpu
from jax.sharding import PartitionSpec as P

D = 2048
FF = 1024
E = 16


beta_first = 0.9
beta_second = 0.95
learn_rate = 0.01
decay_rate = 0.1
adam_eps = 1e-08
bias_first = 1.0 - 0.9**10
bias_second = 1.0 - 0.95**10


def silu_parts(values):
    logistic = jax.nn.sigmoid(values)
    return (values * logistic, logistic * (1.0 + values * (1.0 - logistic)))


def adam_step(weight, moment, square, gradient):
    new_moment = beta_first * moment + (1.0 - beta_first) * gradient
    new_square = beta_second * square + (1.0 - beta_second) * gradient * gradient
    update = (
        new_moment / bias_first / (jnp.sqrt(new_square / bias_second) + adam_eps)
        + decay_rate * weight
    )
    return (weight - learn_rate * update, new_moment, new_square)


def after(value, *earlier):
    return lax.optimization_barrier((value,) + earlier)[0]


def expert_sums(experts, pieces, kept, guests):
    depth, width = pieces[0].shape
    counts = (kept, kept, guests)
    total = sum(counts)
    tile = 16

    def kernel(expert_ref, *refs):
        piece_refs = refs[: len(pieces)]
        out_refs = refs[len(pieces) : -1]
        acc_ref = refs[-1]
        acc_ref[...] = jnp.zeros_like(acc_ref)
        for k, piece_ref in enumerate(piece_refs):
            e = expert_ref[k]
            acc_ref[e] = acc_ref[e] + piece_ref[...].astype(jnp.float32)
        start = 0
        for out_ref, count in zip(out_refs, counts):
            out_ref[...] = acc_ref[start : start + count].astype(out_ref.dtype)
            start += count

    return pl.pallas_call(
        kernel,
        grid_spec=pltpu.PrefetchScalarGridSpec(
            num_scalar_prefetch=1,
            grid=(depth // tile,),
            in_specs=[pl.BlockSpec((tile, width), lambda i, e: (i, 0)) for _ in pieces],
            out_specs=[pl.BlockSpec((c, tile, width), lambda i, e: (0, i, 0)) for c in counts],
            scratch_shapes=[pltpu.VMEM((total, tile, width), jnp.float32)],
        ),
        out_shape=[jax.ShapeDtypeStruct((c, depth, width), jnp.bfloat16) for c in counts],
        compiler_params=pltpu.CompilerParams(vmem_limit_bytes=24 * 1024 * 1024),
        cost_estimate=pl.CostEstimate(
            flops=len(pieces) * depth * width,
            bytes_accessed=2 * (len(pieces) + total) * depth * width,
            transcendentals=0,
        ),
    )(experts, *pieces)


def pick_experts(stack, experts):
    return jnp.take(stack, experts, axis=0, mode="clip")


def place_slots(slot_expert, members):
    slots = slot_expert.shape[0]
    room = slots // 2
    per_plane = E // 2
    most = slots - per_plane
    guests = -(-per_plane * (most - room) // most)
    expert = jnp.clip(slot_expert, 0, E - 1)
    ids = jnp.arange(slots, dtype=jnp.int32)
    kinds = jnp.arange(E, dtype=jnp.int32)
    held = jnp.sum((expert[None, :] == kinds[:, None]).astype(jnp.int32), axis=1)
    kind_home = kinds // per_plane
    ahead = (held[None, :] > held[:, None]) | (
        (held[None, :] == held[:, None]) & (kinds[None, :] < kinds[:, None])
    )
    same = kind_home[None, :] == kind_home[:, None]
    kind_rank = jnp.sum((ahead & same).astype(jnp.int32), axis=1)
    is_kind = (expert[:, None] == kinds[None, :]).astype(jnp.int32)
    rank = jnp.sum(is_kind * kind_rank[None, :], axis=1)
    home = expert // per_plane
    first = (rank[None, :] < rank[:, None]) | (
        (rank[None, :] == rank[:, None]) & (ids[None, :] < ids[:, None])
    )
    before = jnp.sum((first & (home[None, :] == home[:, None])).astype(jnp.int32), axis=1)
    at_home = jnp.sum((home[None, :] == home[:, None]).astype(jnp.int32), axis=1)
    moved = before < at_home - room
    plane = jnp.where(moved, 1 - home, home)
    turn = ids + slots * moved.astype(jnp.int32)
    lower = (plane[None, :] == plane[:, None]) & (turn[None, :] < turn[:, None])
    order_in = jnp.sum(lower.astype(jnp.int32), axis=1)
    side = members // 2
    layer = order_in // (room // 2)
    inner = order_in % (room // 2)
    place = plane * room + inner // side * members + layer * side + inner % side
    early = most - room <= room // 2
    there = (place[None, :] == ids[:, None]).astype(jnp.int32)
    expert_at = jnp.sum(there * expert[None, :], axis=1)
    order = jnp.arange(guests, dtype=jnp.int32)
    tops = [
        jnp.sum(
            jnp.where(
                (kind_rank[None, :] == order[:, None]) & (kind_home[None, :] == p), kinds[None, :], 0
            ),
            axis=1,
        )
        for p in (0, 1)
    ]
    return place, expert_at, tops, guests, early


def exchange(payload, axes, index_groups=None):
    return lax.all_to_all(
        payload, axes, split_axis=0, concat_axis=0, tiled=True, axis_index_groups=index_groups
    )


def on_device(
    tokens,
    cotangent,
    route_weight,
    slot_expert,
    targets,
    proj_in,
    first_in,
    second_in,
    proj_out,
    first_out,
    second_out,
):
    groups = lax.axis_size("grp")
    members = lax.axis_size("dev")
    slot_count = groups * members
    everyone = ("grp", "dev")
    tok_count = tokens.shape[0]
    capacity = 3 * tok_count // slot_count
    side = members // 2
    pair = 2 * capacity
    pair_rows = slot_count * pair
    slot_rows = slot_count * capacity
    wide = D // 2
    part = FF // 2
    swap = [(d, (d + side) % members) for d in range(members)]

    my_group = lax.axis_index("grp")
    my_dev = lax.axis_index("dev")
    high = my_dev >= side
    spot = my_dev % side
    core = my_group % 2
    kept = proj_in.shape[0]
    place, expert_at, tops, guests, early = place_slots(slot_expert, members)
    here = my_group // 2 == 0
    own_top = jnp.where(here, tops[0], tops[1])
    far_top = jnp.where(here, tops[1], tops[0])

    def near_index(experts):
        inner = experts % kept
        return jnp.where(experts // kept == my_group, inner, inner + kept)

    group_expert = lax.dynamic_slice_in_dim(expert_at, my_group * members, members)
    is_guest = group_expert // kept // 2 != my_group // 2
    guest_at = jnp.sum(
        jnp.where(
            group_expert[:, None] == far_top[None, :],
            jnp.arange(guests, dtype=jnp.int32)[None, :],
            0,
        ),
        axis=1,
    )
    source_at = jnp.where(is_guest, 2 * kept + guest_at, near_index(group_expert))
    pair_source = source_at.reshape(2, side).T
    ring = jnp.arange(side, dtype=jnp.int32)
    doubled = jnp.concatenate([pair_source, pair_source], axis=0)
    ahead_source = lax.dynamic_slice_in_dim(doubled, spot, side).reshape(members)
    behind_source = pair_source[(spot - ring) % side].reshape(members)

    core_swap = [(g, g + 1 - 2 * (g % 2)) for g in range(groups)]
    plane_swap = [(g, (g + groups // 2) % groups) for g in range(groups)]

    def to_core(values):
        return lax.ppermute(values, "grp", core_swap)

    def to_plane(values):
        return lax.ppermute(values, "grp", plane_swap)

    def to_spot(values, k):
        shift = [(d, d - d % side + (d % side + k) % side) for d in range(members)]
        return lax.ppermute(values, "dev", shift)

    def row_half(values, index):
        rows = values.shape[1] // 2
        return lax.dynamic_slice_in_dim(values, index * rows, rows, axis=1)

    def join_halves(mine, theirs):
        return jnp.where(
            core == 0,
            jnp.concatenate([mine, theirs], axis=1),
            jnp.concatenate([theirs, mine], axis=1),
        )

    def spread(low):
        near = jnp.concatenate([low, to_core(low)], axis=0)
        guest = to_plane(row_half(pick_experts(near, near_index(own_top)), core))
        far = join_halves(guest, to_core(guest))
        full = jnp.concatenate([near, far], axis=0)
        return [near if early else full, full]

    def to_slot(stack, b):
        picked = [
            lax.dynamic_index_in_dim(stack, ahead_source[2 * k + b], 0, keepdims=False)
            for k in range(side)
        ]
        pieces = [picked[0]] + [to_spot(picked[k], k) for k in range(1, side)]
        held = pick_experts(jnp.stack(pieces), (spot - ring) % side)
        return held.reshape(-1, held.shape[2])

    low_out = proj_out.astype(jnp.bfloat16)
    low_in = proj_in.astype(jnp.bfloat16)
    half = low_in.shape[1] // 2
    all_1 = spread(low_in[:, :half])
    all_2 = spread(low_in[:, half:])
    all_down = spread(low_out)

    slot_target = targets.reshape(-1)
    slot_ids = jnp.arange(slot_count, dtype=jnp.int32)
    flat_target = jnp.sum(
        jnp.where(slot_target[:, None] == slot_ids[None, :], place[None, :], 0), axis=1
    )
    onehot = (flat_target[:, None] == jnp.arange(slot_count, dtype=jnp.int32)[None, :]).astype(
        jnp.int32
    )
    earlier = jnp.cumsum(onehot, axis=0) - onehot
    position = jnp.sum(earlier * onehot, axis=1)
    within = position < capacity
    member = flat_target % members
    host = flat_target - member + member % side
    row = host * pair + (member // side) * capacity + position
    row = jnp.where(within, row, -2 * pair_rows).reshape(tok_count, 2)
    rows_of = [[row[:, k] + h * side * pair for k in (0, 1)] for h in (0, 1)]
    places = jnp.arange(pair_rows, dtype=jnp.int32)

    def hits(wanted):
        found = places[:, None] == wanted[0][None, :]
        for other in wanted[1:]:
            found = found | (places[:, None] == other[None, :])
        return found

    def takes(wanted):
        found = wanted[0][:, None] == places[None, :]
        for other in wanted[1:]:
            found = found | (other[:, None] == places[None, :])
        return found

    def by_chunk(values):
        split = values.reshape(tok_count, 2, side, 2, half)
        return jnp.swapaxes(split, 2, 3).reshape(tok_count, D)

    def from_chunk(values):
        split = values.reshape(tok_count, 2, 2, side, half)
        return jnp.swapaxes(split, 2, 3).reshape(tok_count, D)

    picker_x = jnp.concatenate([hits(rows_of[0]), hits(rows_of[1])], axis=1).astype(jnp.bfloat16)
    picker_dy = jnp.concatenate(
        [hits([rows_of[0][k], rows_of[1][k]]) for k in (0, 1)], axis=1
    ).astype(jnp.bfloat16)
    cot_float = cotangent.astype(jnp.float32)
    scaled = [(route_weight[:, k : k + 1] * cot_float).astype(jnp.bfloat16) for k in (0, 1)]
    chunked = by_chunk(tokens)
    send_x = jnp.dot(
        picker_x,
        jnp.concatenate([chunked[:, :wide], chunked[:, wide:]], axis=0),
        preferred_element_type=jnp.float32,
    ).astype(jnp.bfloat16)
    send_dy = jnp.dot(
        picker_dy, jnp.concatenate(scaled, axis=0), preferred_element_type=jnp.float32
    ).astype(jnp.bfloat16)
    send = jnp.concatenate([send_x, send_dy], axis=1)
    slot_both = exchange(send.reshape(slot_count, pair, wide + D), everyone)

    up_1, up_2, slot_down = [], [], []
    for b in (0, 1):
        up_1.append(to_slot(all_1[b], b))
        up_2.append(to_slot(all_2[b], b))
        slot_down.append(to_slot(all_down[b], b))

    across = (((1,), (1,)), ((), ()))
    down = (((0,), (0,)), ((), ()))

    def low_dot(a, b, dims):
        return lax.dot_general(a, b, dims, preferred_element_type=jnp.float32).astype(jnp.bfloat16)

    def pass_over(values):
        return lax.ppermute(values, "dev", swap)

    both = (0, 1)
    quarter = side * half
    slot_x = [slot_both[:, b * capacity : (b + 1) * capacity, :wide].reshape(slot_rows, wide) for b in both]
    slot_dy = [slot_both[:, b * capacity : (b + 1) * capacity, wide:].reshape(slot_rows, D) for b in both]
    x_1 = [x[:, :quarter] for x in slot_x]
    x_2 = [x[:, quarter:] for x in slot_x]

    def turned(values):
        width = values.shape[1] // side
        twice = jnp.concatenate([values, values], axis=1)
        return lax.dynamic_slice_in_dim(twice, spot * width, values.shape[1], axis=1)

    dhidden = [
        lax.dot_general(slot_dy[b], slot_down[b], across, preferred_element_type=jnp.float32)
        for b in both
    ]
    mine = []
    passed = []
    for b in both:
        total = jnp.dot(x_1[b], up_1[b], preferred_element_type=jnp.float32) + jnp.dot(
            x_2[b], up_2[b], preferred_element_type=jnp.float32
        )
        lower = jnp.concatenate([total[:, :part], total[:, FF : FF + part]], axis=1)
        upper = jnp.concatenate([total[:, part:FF], total[:, FF + part :]], axis=1)
        mine.append(jnp.where(high, upper, lower))
        theirs = jnp.where(high, lower, upper).astype(jnp.bfloat16)
        passed.append(pass_over(theirs))
    hidden = []
    grad_gateup = []
    for b in both:
        gate_up = mine[b] + passed[b].astype(jnp.float32)
        upward = gate_up[:, part:]
        active, derivative = silu_parts(gate_up[:, :part])
        hidden.append((active * upward).astype(jnp.bfloat16))
        own = jnp.concatenate(
            [dhidden[b] * upward * derivative, dhidden[b] * active], axis=1
        ).astype(jnp.bfloat16)
        other = pass_over(own)
        lower = jnp.where(high, other, own)
        upper = jnp.where(high, own, other)
        grad_gateup.append(
            jnp.concatenate(
                [lower[:, :part], upper[:, :part], lower[:, part:], upper[:, part:]], axis=1
            )
        )

    def to_owners(grad):
        rows = grad.shape[0] // side
        pieces = [grad[k * rows : (k + 1) * rows] for k in range(side)]
        return [pieces[0]] + [to_spot(pieces[k], k) for k in range(1, side)]

    def sent(grads):
        moved = []
        for b in both:
            moved.append(to_owners(grads[b]))
        return [moved[b][k] for k in range(side) for b in both]

    def collect(pieces):
        own, other, guest = expert_sums(behind_source, pieces, kept, guests)
        near = to_core(other)
        share = row_half(guest, core).astype(jnp.float32) + to_core(
            row_half(guest, 1 - core)
        ).astype(jnp.float32)
        home = to_plane(share.astype(jnp.bfloat16))
        return own, near, home, to_core(home)

    def add_up(own, near, home, theirs):
        back_home = join_halves(home, theirs).astype(jnp.float32)
        mine = jnp.arange(kept, dtype=jnp.int32) + my_group * kept
        total = own.astype(jnp.float32) + near.astype(jnp.float32)
        for k in range(guests):
            total = total + jnp.where((mine == own_top[k])[:, None, None], back_home[k][None], 0.0)
        return total.astype(jnp.bfloat16)

    late_hidden = [after(hidden[b], slot_down[b]) for b in both]
    grad_down = [low_dot(turned(late_hidden[b]), slot_dy[b], down) for b in both]
    rows_down = sent(grad_down)
    result = [low_dot(hidden[b], slot_down[b], (((1,), (0,)), ((), ()))) for b in both]
    grad_1 = [low_dot(turned(x_1[b]), grad_gateup[b], down) for b in both]
    rows_1 = sent(grad_1)
    grad_2 = [low_dot(turned(x_2[b]), grad_gateup[b], down) for b in both]
    rows_2 = sent(grad_2)
    rows_back = [
        jnp.concatenate(
            [
                low_dot(grad_gateup[b], up_1[b], across),
                low_dot(grad_gateup[b], up_2[b], across),
                result[b],
            ],
            axis=1,
        ).reshape(slot_count, capacity, wide + D)
        for b in both
    ]
    back = jnp.concatenate(rows_back, axis=1)
    back = exchange(back, everyone).reshape(pair_rows, wide + D)
    sum_down = add_up(*collect(rows_down))
    sum_1 = add_up(*collect(rows_1))
    sum_2 = add_up(*collect(rows_2))
    sum_up = jnp.concatenate([sum_1, sum_2], axis=1)

    taker = jnp.concatenate(
        [takes([rows_of[0][k], rows_of[1][k]]) for k in (0, 1)], axis=0
    ).astype(jnp.bfloat16)
    taken = jnp.dot(taker, back[:, wide:], preferred_element_type=jnp.float32).astype(jnp.bfloat16)
    out_0 = taken[:tok_count].astype(jnp.float32)
    out_1 = taken[tok_count:].astype(jnp.float32)
    taker_dx = jnp.concatenate([takes(rows_of[0]), takes(rows_of[1])], axis=0).astype(jnp.bfloat16)
    taken_dx = jnp.dot(taker_dx, back[:, :wide], preferred_element_type=jnp.float32)
    mixed = (route_weight[:, 0:1] * out_0 + route_weight[:, 1:2] * out_1).astype(jnp.bfloat16)
    token_grad = from_chunk(
        jnp.concatenate([taken_dx[:tok_count], taken_dx[tok_count:]], axis=1).astype(jnp.bfloat16)
    )
    mix_grad = jnp.stack(
        [jnp.sum(cot_float * out_0, axis=1), jnp.sum(cot_float * out_1, axis=1)], axis=1
    )

    trained_in, mean_in, square_in = adam_step(
        proj_in, first_in, second_in, sum_up.astype(jnp.float32)
    )
    trained_out, mean_out, square_out = adam_step(
        proj_out, first_out, second_out, sum_down.astype(jnp.float32)
    )
    return (
        mixed,
        token_grad,
        mix_grad,
        trained_in,
        mean_in,
        square_in,
        trained_out,
        mean_out,
        square_out,
    )


def solution(mesh):
    in_specs = (
        P(("grp", "dev"), None),
        P(("grp", "dev"), None),
        P(("grp", "dev"), None),
        P(),
        P(("grp", "dev"), None),
        P("grp", "dev", None),
        P("grp", "dev", None),
        P("grp", "dev", None),
        P("grp", "dev", None),
        P("grp", "dev", None),
        P("grp", "dev", None),
    )
    out_specs = (
        P(("grp", "dev"), None),
        P(("grp", "dev"), None),
        P(("grp", "dev"), None),
        P("grp", "dev", None),
        P("grp", "dev", None),
        P("grp", "dev", None),
        P("grp", "dev", None),
        P("grp", "dev", None),
        P("grp", "dev", None),
    )
    return jax.shard_map(
        on_device, mesh=mesh, in_specs=in_specs, out_specs=out_specs, check_vma=False
    )
```
